128 devices in a mesh: row: 8 (over z_lo, x), col: 16 (over y, z_hi, core).
Axes of the slice: x: 4, y: 4, z: 4 (z_hi: 2, z_lo: 2; z = z_hi * 2 + z_lo), core: 2. Of those that a mesh axis runs over, the one named last changes fastest.
Arguments:
- beats: bfloat16 [262144, 128], P(('row', 'col')), may hold values from -6 to 6
- track_marks: int32 [262144], P(('row', 'col')), may hold values 0 or 1
- valid_beats: int32 [128], replicated, may hold values from 64 to 2048, as said below
- pairing: int32 [2, 128], replicated, may hold values from 0 to 127, as said below
Outputs:
- profile: float32 [262144], P(('row', 'col'))
The draws below stay inside these ranges and needn't reach their ends.
Inputs may be any that keep to these rules, and one draw needn't show every extreme that they name: `valid_beats`: each segment has at least 64 valid beats; some segment is full in every draw. pairing[0] pairs the segments of each grid column among themselves and pairing[1] those of each grid row; each row of pairing is an involution without fixed points.
All inputs are finite; a program needn't handle non-finite values. No bound on the sum of `track_marks` on one device may be relied on, other than what follows from the above.
Results may differ from the reference program's by a relative error of at most 0.0003.
Values may be sent and summed in bfloat16 or wider, within the bound.
No kernel may reach another device: no remote copies, remote signals or barrier semaphores. Data moves between devices by JAX's collectives and lax.ppermute only.
A program may use at most 128 MiB of HBM per device.

```python
import jax
import jax.numpy as jnp
from jax import lax

WIDTH = 128
SPAN = 64
SEG_BEATS = 2048
ROW_SEGS = 8
COL_SEGS = 16
SEGS = 128
BEATS = 262144


def draw_valid_beats(key, part):
    counts = jax.random.randint(jax.random.fold_in(key, 11), (SEGS,), SPAN, SEG_BEATS)
    whole = jax.random.randint(jax.random.fold_in(key, 12), (SEGS,), 0, 2)
    counts = jnp.where(whole == 1, SEG_BEATS, counts)
    return counts.at[0].set(SEG_BEATS).astype(jnp.int32)


def pair_within(key, groups, members):
    keys = jax.random.split(key, groups)
    orders = jax.vmap(lambda single: jax.random.permutation(single, members))(keys)
    mates = orders[:, jnp.arange(members) ^ 1]
    result = jnp.zeros((groups, members), jnp.int32)
    group_ids = jnp.arange(groups)[:, None] * jnp.ones((1, members), jnp.int32)
    return result.at[group_ids, orders].set(mates.astype(jnp.int32))


def draw_pairing(key, part):
    column_mates = pair_within(jax.random.fold_in(key, 21), COL_SEGS, ROW_SEGS)
    row_mates = pair_within(jax.random.fold_in(key, 22), ROW_SEGS, COL_SEGS)
    grid_rows = jnp.arange(ROW_SEGS, dtype=jnp.int32)[:, None]
    grid_cols = jnp.arange(COL_SEGS, dtype=jnp.int32)[None, :]
    first = column_mates.T * COL_SEGS + grid_cols
    second = grid_rows * COL_SEGS + row_mates
    return jnp.stack([first.reshape(SEGS), second.reshape(SEGS)], 0).astype(jnp.int32)


def touch_ends(drawn, own_key, smallest, largest):
    spot = [jax.random.randint(jax.random.fold_in(own_key, axis), (), 0, length) for axis, length in enumerate(drawn.shape)]
    widest = drawn.shape.index(max(drawn.shape))
    next_to = spot[:widest] + [(spot[widest] + 1) % drawn.shape[widest]] + spot[widest + 1:]
    return drawn.at[tuple(spot)].set(smallest).at[tuple(next_to)].set(largest)


def block_levels(stream_key, extent, cuts, least, top_value):
    def one(dim, parts):
        steps = jax.random.uniform(jax.random.fold_in(jax.random.fold_in(stream_key, 6), dim), (parts,), jnp.float32, least / len(cuts), top_value / len(cuts))
        return jnp.repeat(jnp.exp(steps), extent[dim] // parts).reshape((-1,) + (1,) * (len(extent) - dim - 1))

    level = one(*cuts[0])
    for cut in cuts[1:]:
        level = level * one(*cut)
    return level


def centred(stream_key, shape, deviation, reach, cuts=(), kind=jnp.bfloat16):
    loudness = block_levels(stream_key, shape, cuts, -0.22, 0.18) if cuts else 1.0
    drawn = jax.random.normal(stream_key, shape, jnp.float32) * deviation * loudness
    return jnp.minimum(jnp.maximum(drawn, -reach), reach).astype(kind)


def setup_inputs(seed: int = 0) -> dict:
    key_of = jax.random.split(jax.random.key(seed), 5)
    beats = centred(key_of[0], (BEATS, WIDTH), 1.0, 6.0, ((0, 128),))
    track_marks = touch_ends((jax.random.randint(key_of[1], (BEATS,), 0, 256) < 1).astype(jnp.int32), jax.random.fold_in(key_of[1], 1), 0, 1)
    valid_beats = draw_valid_beats(jax.random.fold_in(key_of[4], 71), 0)
    pairing = draw_pairing(jax.random.fold_in(key_of[4], 71), 0)
    return dict(beats=beats, track_marks=track_marks, valid_beats=valid_beats, pairing=pairing)


CEIL = 4.0


def window_sum(values):
    total = values[..., 0:SEG_BEATS]
    for shift in range(1, SPAN):
        total = total + values[..., shift:shift + SEG_BEATS]
    return total


def reference(beats, track_marks, valid_beats, pairing):
    seg_beats = beats.reshape(SEGS, SEG_BEATS, WIDTH)
    following = jnp.concatenate([seg_beats[1:, :SPAN], jnp.zeros((1, SPAN, WIDTH), beats.dtype)], 0)
    extended = jnp.concatenate([seg_beats, following], 1).astype(jnp.float32)
    marks = track_marks.astype(jnp.float32).reshape(SEGS, SEG_BEATS)
    mark_next = jnp.concatenate([marks[1:, :SPAN], jnp.zeros((1, SPAN), jnp.float32)], 0)
    mark_ext = jnp.concatenate([marks, mark_next], 1)
    crossed = mark_ext[:, 1:1 + SEG_BEATS]
    for shift in range(2, SPAN):
        crossed = crossed + mark_ext[:, shift:shift + SEG_BEATS]
    offsets = jnp.arange(SEG_BEATS, dtype=jnp.int32)
    segment_ids = jnp.arange(SEGS, dtype=jnp.int32)
    within = offsets[None, :] + (SPAN - 1) < valid_beats[:, None]
    crossing = (valid_beats == SEG_BEATS) & (segment_ids < SEGS - 1)
    live = (within | crossing[:, None]) & (crossed < 0.5)
    norms = window_sum(jnp.sum(extended * extended, axis=2))

    def row_minima(owner, other):
        left = extended[owner, :SEG_BEATS + SPAN - 1]
        right = extended[other, :SEG_BEATS + SPAN - 1]
        gram = jnp.dot(left, right.T, precision=lax.Precision.HIGHEST)

        def accumulate(shift, total):
            return total + lax.dynamic_slice(gram, (shift, shift), (SEG_BEATS, SEG_BEATS))

        dots = lax.fori_loop(0, SPAN, accumulate, jnp.zeros((SEG_BEATS, SEG_BEATS), jnp.float32))
        dist = (norms[owner][:, None] + norms[other][None, :] - 2.0 * dots) / (SPAN * WIDTH)
        pos_own = (owner * SEG_BEATS + offsets).astype(jnp.int32)
        pos_other = (other * SEG_BEATS + offsets).astype(jnp.int32)
        allowed = live[owner][:, None] & live[other][None, :] & (jnp.abs(pos_own[:, None] - pos_other[None, :]) >= SPAN // 2)
        return jnp.min(jnp.where(allowed, dist, CEIL), axis=1)

    def one_segment(owner):
        first = row_minima(owner, pairing[0, owner])
        second = row_minima(owner, pairing[1, owner])
        return jnp.minimum(first, second)

    profile = lax.map(one_segment, segment_ids)
    return profile.reshape(BEATS)
```

```python
import functools

import jax
import jax.numpy as jnp
from jax import lax
from jax.experimental import pallas as pl
from jax.experimental.pallas import tpu as pltpu
from jax.sharding import PartitionSpec as P

WIDTH = 128
SPAN = 64
CEIL = 4.0
SEG = 2048
DEVS = 128
LANES = 128
SUBS = 8
STEP = SEG // SUBS
FOLD = 17
WRAP = FOLD * LANES
CHUNK = 16
SLOT1 = 24
SLOT2 = 40
DEAD = float(2**24)
F32 = jnp.float32
BF16 = jnp.bfloat16
VMEM = pltpu.VMEM


def scatter_kernel(beats_ref, marks_ref, out_ref, wide, flags):
    wide[0:SEG, :] = beats_ref[...].astype(F32)
    marks = marks_ref[...].astype(F32)
    flags[...] = marks
    pad = jnp.zeros((LANES - 2 * SUBS, LANES), F32)
    sub = lax.broadcasted_iota(jnp.int32, (SUBS, LANES), 0)
    turned = []
    for half in range(2):
        block = flags[pl.ds(half, SUBS, stride=2), :]
        extra = jnp.where(sub == 0, block, 0.0)
        turned.append(jnp.transpose(jnp.concatenate([block, extra, pad], 0)))
    flags2 = jnp.concatenate(turned, 0)
    out_ref[:, CHUNK:SLOT1, :] = jnp.zeros((DEVS, SUBS, LANES), BF16)
    wide[pl.ds(SEG, 2 * LANES), :] = flags2

    def one(k, _):
        first = wide[pl.ds(2 * k, SUBS, stride=STEP), :]
        second = wide[pl.ds(2 * k + 1, SUBS, stride=STEP), :]
        out_ref[k, 0:CHUNK, :] = jnp.concatenate([first, second], 0).astype(BF16)
        mark0 = wide[pl.ds(SEG + 2 * k, SUBS, stride=0), :]
        mark1 = wide[pl.ds(SEG + 2 * k + 1, SUBS, stride=0), :]
        beat0 = wide[pl.ds(2 * k, SUBS, stride=0), :]
        beat1 = wide[pl.ds(2 * k + 1, SUBS, stride=0), :]
        even = jnp.where(sub < 4, mark0, beat0)
        odd = jnp.where(sub < 4, mark1, beat1)
        rest = jnp.where((sub & 1) == 0, even, odd)
        out_ref[k, CHUNK:SLOT1, :] = rest.astype(BF16)
        return 0

    lax.fori_loop(0, DEVS, one, 0, unroll=4)


def route_kernel(pick_ref, got_ref, out_ref):
    sub = lax.broadcasted_iota(jnp.int32, (SUBS, LANES), 0)
    lane = lax.broadcasted_iota(jnp.int32, (SUBS, LANES), 1)
    marks = (sub < 4) & (lane < SUBS)
    to_first = ((sub < 4) & (sub < 2)) | (sub == 4) | (sub == 5)

    def one(d, _):
        first, second = pick_ref[0, d], pick_ref[1, d]
        after1, after2 = pick_ref[2, d], pick_ref[3, d]
        out_ref[d, 0:CHUNK, :] = got_ref[first, 0:CHUNK, :]
        out_ref[d, CHUNK : 2 * CHUNK, :] = got_ref[second, 0:CHUNK, :]
        mark1 = got_ref[first, CHUNK:SLOT1, :].astype(F32)
        mark2 = got_ref[second, CHUNK:SLOT1, :].astype(F32)
        next1 = got_ref[after1, CHUNK:SLOT1, :].astype(F32)
        next2 = got_ref[after2, CHUNK:SLOT1, :].astype(F32)
        own = jnp.where(to_first, mark1, mark2)
        behind = jnp.where(to_first, next1, next2)
        out_ref[d, 2 * CHUNK : SLOT2, :] = jnp.where(marks, own, behind).astype(BF16)
        return 0

    lax.fori_loop(0, DEVS, one, 0, unroll=4)


def join_kernel(info_ref, got_ref, own_ref, head_ref, out_ref, wide, right, left, prod, squares, extra, gates, bias):
    sub = lax.broadcasted_iota(jnp.int32, (SUBS, LANES), 0)
    lane = lax.broadcasted_iota(jnp.int32, (SUBS, LANES), 1)
    me = info_ref[0]

    wide[0:SPAN, :] = jnp.zeros((SPAN, LANES), F32)
    wide[pl.ds(SPAN, SEG), :] = own_ref[...].astype(F32)
    wide[pl.ds(SPAN + SEG, SPAN), :] = head_ref[0:SPAN, :].astype(F32)
    wide[pl.ds(2 * SPAN + SEG, SPAN), :] = jnp.zeros((SPAN, LANES), F32)
    for j in range(FOLD):
        here = wide[pl.ds(SPAN + j, LANES, stride=FOLD), :]
        back = wide[pl.ds(j, LANES, stride=FOLD), :]
        right[j * LANES : (j + 1) * LANES, 0:LANES] = (here * -2.0).astype(BF16)
        right[j * LANES : (j + 1) * LANES, LANES:] = (back * 2.0).astype(BF16)

    def widen(k, _):
        extra[pl.ds(pl.multiple_of(k * SUBS, SUBS), SUBS), :] = got_ref[k, 2 * CHUNK : SLOT2, :].astype(F32)
        return 0

    lax.fori_loop(0, DEVS, widen, 0, unroll=4)
    left[0 : SPAN * SUBS, LANES:] = jnp.zeros((SPAN * SUBS, LANES), BF16)

    row = lax.broadcasted_iota(jnp.int32, (STEP, LANES), 0)
    column = lax.broadcasted_iota(jnp.int32, (STEP, LANES), 1)

    def band(offset):
        gap = 2 * column + offset - row
        return jnp.where((gap >= 1) & (gap < SPAN), 1.0, 0.0).astype(BF16)

    bands = jnp.concatenate([band(0), band(1), band(STEP), band(STEP + 1)], 1)
    place = STEP * column + row
    base = FOLD * lane - STEP * sub

    bias[SEG:, :] = jnp.full((SUBS, LANES), 3.0e38, F32)
    best = [jnp.full((SUBS, LANES), 3.0e38, F32) for _ in range(FOLD)]
    for part in range(2):
        partner, valid, crossing = info_ref[1 + part], info_ref[3 + part], info_ref[5 + part]

        even = extra[pl.ds(2 * part, DEVS, stride=SUBS), :]
        odd = extra[pl.ds(2 * part + 1, DEVS, stride=SUBS), :]
        marks = jnp.concatenate(
            [even, odd, pltpu.roll(even, LANES - 1, 1), pltpu.roll(odd, LANES - 1, 1)], 0
        ).astype(BF16)
        crossed = jnp.dot(bands, marks, preferred_element_type=F32)
        live = ((place + (SPAN - 1) < valid) | (crossing > 0)) & (crossed < 0.5)
        gates[0:STEP, :] = jnp.where(live, 0.0, DEAD)

        def fill(k, _, part=part):
            rows = got_ref[k, part * CHUNK : (part + 1) * CHUNK, :]
            at = pl.multiple_of(k * CHUNK, CHUNK)
            left[pl.ds(at, CHUNK), 0:LANES] = rows
            left[pl.ds(at + SPAN * SUBS, CHUNK), LANES:] = rows
            x = rows.astype(F32)
            squares[pl.ds(at, CHUNK), :] = x * x
            return 0

        lax.fori_loop(0, DEVS, fill, 0, unroll=4)

        def follow(k, _, part=part):
            x = got_ref[k, part * CHUNK : (part + 1) * CHUNK, :].astype(F32)
            halves = []
            for half in range(2):
                behind = extra[pl.ds(k * SUBS + 4 + 2 * part + half, SUBS, stride=0), :]
                moved = pltpu.roll(x[half * SUBS : (half + 1) * SUBS], SUBS - 1, 0)
                halves.append(jnp.where(sub == SUBS - 1, behind, moved))
            y = jnp.concatenate(halves, 0)
            at = pl.multiple_of(SEG + k * CHUNK, CHUNK)
            left[pl.ds(at, CHUNK), 0:LANES] = y.astype(BF16)
            squares[pl.ds(at, CHUNK), :] = y * y
            return 0

        lax.fori_loop(0, SPAN // 2, follow, 0, unroll=4)

        def square(u):
            return squares[pl.ds(pl.multiple_of(u * SUBS, SUBS), SUBS), :]

        start = lax.fori_loop(
            0, SPAN, lambda u, t: t + square(u), jnp.zeros((SUBS, LANES), F32), unroll=8
        )

        def norm(i, total):
            gate = jnp.where(sub == lane, gates[pl.ds(i, SUBS, stride=0), :], 0.0)
            flat = jnp.sum(total + gate, axis=1, keepdims=True)
            bias[pl.ds(pl.multiple_of(i * SUBS, SUBS), SUBS), :] = jnp.broadcast_to(flat, (SUBS, LANES))
            return total + (square(i + SPAN) - square(i))

        lax.fori_loop(0, STEP, norm, start, unroll=8)

        shift = base + (me - partner) * SEG

        def block(b, carry, keep):
            at = pl.multiple_of(b * 256, 256)
            prod[...] = lax.dot_general(
                left[pl.ds(at, 256), :], right[...], (((1,), (1,)), ((), ())), preferred_element_type=F32
            )

            def eight(g, carry):
                for r in range(8):
                    total, low = carry
                    total = [pltpu.roll(total[-1], 1, 1)] + list(total[:-1])
                    rows = pl.ds(pl.multiple_of((g * 8 + r) * SUBS, SUBS), SUBS)
                    total = [total[j] + prod[rows, j * LANES : (j + 1) * LANES] for j in range(FOLD)]
                    low = list(low)
                    i = b * 32 + g * 8 + r - (SPAN - 1)
                    if keep == "all" or keep == "masked":
                        add = bias[pl.ds(pl.multiple_of(i * SUBS, SUBS), SUBS), :]
                        for j in range(FOLD):
                            value = total[j] + add
                            if keep == "masked":
                                gap = shift + (j - (SPAN - 1) - i)
                                value = jnp.where(jnp.abs(gap) < SPAN // 2, 3.0e38, value)
                            low[j] = jnp.minimum(low[j], value)
                    carry = (total, low)
                return carry

            return lax.fori_loop(0, 4, eight, carry)

        total = [jnp.zeros((SUBS, LANES), F32) for _ in range(FOLD)]

        def last(carry):
            total, low = carry
            add = bias[0:SUBS, :]
            low = list(low)
            for j in range(FOLD):
                gap = shift + (j - (SPAN - 1))
                value = jnp.where(jnp.abs(gap) < SPAN // 2, 3.0e38, total[j] + add)
                low[j] = jnp.minimum(low[j], value)
            return (total, low)

        carry = (total, best)
        carry = lax.fori_loop(0, 2, lambda b, c: block(b, c, "none"), carry)
        carry = last(carry)
        carry = block(2, carry, "masked")
        carry = lax.fori_loop(3, 9, lambda b, c: block(b, c, "all"), carry)
        carry = block(9, carry, "masked")
        best = carry[1]

    for j in range(FOLD):
        out_ref[j : j + 1, :] = jnp.min(best[j], axis=0, keepdims=True)


def window_sum(values, count):
    total = values[0:count]
    for shift in range(1, SPAN):
        total = total + values[shift : shift + count]
    return total


def per_device(beats, track_marks, valid_beats, pairing):
    me = lax.axis_index("row") * lax.axis_size("col") + lax.axis_index("col")
    tail = pltpu.CompilerParams(vmem_limit_bytes=48 * 2**20)

    heads = jnp.concatenate(
        [beats[:SPAN], jnp.broadcast_to(track_marks[None, :LANES].astype(BF16), (SUBS, LANES))], 0
    )
    head = lax.ppermute(heads, ("row", "col"), [(i + 1, i) for i in range(DEVS - 1)])

    sent = pl.pallas_call(
        scatter_kernel,
        out_shape=jax.ShapeDtypeStruct((DEVS, SLOT1, LANES), BF16),
        in_specs=[pl.BlockSpec(memory_space=VMEM)] * 2,
        out_specs=pl.BlockSpec(memory_space=VMEM),
        scratch_shapes=[VMEM((SEG + 2 * LANES + SUBS, LANES), F32), VMEM((CHUNK, LANES), F32)],
        compiler_params=tail,
    )(beats, track_marks.reshape(CHUNK, LANES))
    spread = lax.all_to_all(sent, ("row", "col"), 0, 0, tiled=True)

    after = jnp.minimum(pairing + 1, DEVS - 1)
    routed = pl.pallas_call(
        route_kernel,
        out_shape=jax.ShapeDtypeStruct((DEVS, SLOT2, LANES), BF16),
        in_specs=[pl.BlockSpec(memory_space=pltpu.SMEM), pl.BlockSpec(memory_space=VMEM)],
        out_specs=pl.BlockSpec(memory_space=VMEM),
        compiler_params=tail,
    )(jnp.concatenate([pairing, after], 0), spread)
    got = lax.all_to_all(routed, ("row", "col"), 0, 0, tiled=True)

    partners = pairing[:, me]
    valid = valid_beats[partners]
    crossing = ((valid == SEG) & (partners < DEVS - 1)).astype(jnp.int32)
    info = jnp.concatenate([me[None].astype(jnp.int32), partners, valid, crossing], 0)
    lowest = pl.pallas_call(
        join_kernel,
        out_shape=jax.ShapeDtypeStruct((FOLD, LANES), F32),
        in_specs=[pl.BlockSpec(memory_space=pltpu.SMEM)] + [pl.BlockSpec(memory_space=VMEM)] * 3,
        out_specs=pl.BlockSpec(memory_space=VMEM),
        scratch_shapes=[
            VMEM((SEG + 3 * SPAN, LANES), F32),
            VMEM((WRAP, 2 * LANES), BF16),
            VMEM((SEG + SPAN * SUBS, 2 * LANES), BF16),
            VMEM((256, WRAP), F32),
            VMEM((SEG + SPAN * SUBS, LANES), F32),
            VMEM((DEVS * SUBS + SUBS, LANES), F32),
            VMEM((STEP + SUBS, LANES), F32),
            VMEM((SEG + SUBS, LANES), F32),
        ],
        compiler_params=tail,
    )(info, got, beats, head)

    own_sq = jnp.concatenate(
        [
            jnp.sum(jnp.square(beats.astype(F32)), axis=1),
            jnp.sum(jnp.square(head[:SPAN].astype(F32)), axis=1),
        ],
        0,
    )
    norm = window_sum(own_sq, SEG)
    marks = jnp.concatenate([track_marks.astype(F32), head[SPAN, :SPAN].astype(F32)], 0)
    crossed = marks[1 : 1 + SEG]
    for shift in range(2, SPAN):
        crossed = crossed + marks[shift : shift + SEG]
    offsets = jnp.arange(SEG, dtype=jnp.int32)
    within = offsets + (SPAN - 1) < valid_beats[me]
    over = (valid_beats[me] == SEG) & (me < DEVS - 1)
    live = (within | over) & (crossed < 0.5)
    flat = lowest.T.reshape(WRAP)[SPAN - 1 : SPAN - 1 + SEG]
    dist = (norm + flat) * (1.0 / (SPAN * WIDTH))
    return jnp.where(live, jnp.minimum(dist, CEIL), CEIL)


def solution(mesh):
    placed = (P(("row", "col"), None), P(("row", "col")), P(), P())
    return jax.shard_map(
        per_device, mesh=mesh, in_specs=placed, out_specs=P(("row", "col")), check_vma=False
    )
```

```python
import functools

import jax
import jax.numpy as jnp
from jax import lax
from jax.experimental import pallas as pl
from jax.experimental.pallas import tpu as pltpu
from jax.sharding import PartitionSpec as P

WIDTH = 128
SPAN = 64
CEIL = 4.0
SEG = 2048
DEVS = 128
LANES = 128
SUBS = 8
STEP = SEG // SUBS
FOLD = 17
WRAP = FOLD * LANES
CHUNK = 16
SLOT = 24
SLOT2 = 40
EARLY = True
BLOCK = 512
DEAD = float(2**24)
F32 = jnp.float32
BF16 = jnp.bfloat16
VMEM = pltpu.VMEM


def scatter_kernel(beats_ref, marks_ref, out_ref, wide, flags):
    wide[0:SEG, :] = beats_ref[...].astype(F32)
    marks = marks_ref[...].astype(F32)
    flags[...] = marks
    pad = jnp.zeros((LANES - 2 * SUBS, LANES), F32)
    sub = lax.broadcasted_iota(jnp.int32, (SUBS, LANES), 0)
    turned = []
    for half in range(2):
        block = flags[pl.ds(half, SUBS, stride=2), :]
        extra = jnp.where(sub == 0, block, 0.0)
        turned.append(jnp.transpose(jnp.concatenate([block, extra, pad], 0)))
    flags2 = jnp.concatenate(turned, 0)
    out_ref[:, CHUNK:SLOT, :] = jnp.zeros((DEVS, SUBS, LANES), BF16)
    wide[pl.ds(SEG, 2 * LANES), :] = flags2

    def one(k, _):
        first = wide[pl.ds(2 * k, SUBS, stride=STEP), :]
        second = wide[pl.ds(2 * k + 1, SUBS, stride=STEP), :]
        out_ref[k, 0:CHUNK, :] = jnp.concatenate([first, second], 0).astype(BF16)
        mark0 = wide[pl.ds(SEG + 2 * k, SUBS, stride=0), :]
        mark1 = wide[pl.ds(SEG + 2 * k + 1, SUBS, stride=0), :]
        beat0 = wide[pl.ds(2 * k, SUBS, stride=0), :]
        beat1 = wide[pl.ds(2 * k + 1, SUBS, stride=0), :]
        even = jnp.where(sub < 4, mark0, beat0)
        odd = jnp.where(sub < 4, mark1, beat1)
        rest = jnp.where((sub & 1) == 0, even, odd)
        out_ref[k, CHUNK:SLOT, :] = rest.astype(BF16)
        return 0

    lax.fori_loop(0, DEVS, one, 0, unroll=4)


def route_kernel(pick_ref, got_ref, info_ref, right_ref, norm_ref, out_ref):
    sub = lax.broadcasted_iota(jnp.int32, (SUBS, LANES), 0)
    lane = lax.broadcasted_iota(jnp.int32, (SUBS, LANES), 1)
    marks = (sub < 4) & (lane < SUBS)
    to_first = (sub < 2) | (sub == 4) | (sub == 5)
    to_even = (sub & 1) == 0

    def one(d, _):
        first, second = pick_ref[0, d], pick_ref[1, d]
        after1, after2 = pick_ref[2, d], pick_ref[3, d]
        x = got_ref[first, 0:CHUNK, :].astype(F32)
        y = got_ref[second, 0:CHUNK, :].astype(F32)
        near, far = [], []
        for half in range(2):
            rows = slice(half * SUBS, (half + 1) * SUBS)
            near.append(jnp.where(to_even, x[rows], pltpu.roll(y[rows], 1, 0)))
            far.append(jnp.where(to_even, pltpu.roll(x[rows], SUBS - 1, 0), y[rows]))
        out_ref[d, 0:CHUNK, :] = jnp.concatenate(near, 0).astype(BF16)
        out_ref[d, CHUNK : 2 * CHUNK, :] = jnp.concatenate(far, 0).astype(BF16)
        mark1 = got_ref[first, CHUNK:SLOT, :].astype(F32)
        mark2 = got_ref[second, CHUNK:SLOT, :].astype(F32)
        next1 = got_ref[after1, CHUNK:SLOT, :].astype(F32)
        next2 = got_ref[after2, CHUNK:SLOT, :].astype(F32)
        own = jnp.where(to_first, mark1, mark2)
        behind = jnp.where(to_first, next1, next2)
        out_ref[d, 2 * CHUNK : SLOT2, :] = jnp.where(marks, own, behind).astype(BF16)
        return 0

    lax.fori_loop(0, DEVS, one, 0, unroll=4)


def own_kernel(own_ref, head_ref, out_ref, wide):
    wide[0:SPAN, :] = jnp.zeros((SPAN, LANES), F32)
    wide[pl.ds(SPAN, SEG), :] = own_ref[...].astype(F32)
    wide[pl.ds(SPAN + SEG, SPAN), :] = head_ref[0:SPAN, :].astype(F32)
    wide[pl.ds(2 * SPAN + SEG, SPAN), :] = jnp.zeros((SPAN, LANES), F32)
    for j in range(FOLD):
        here = wide[pl.ds(SPAN + j, LANES, stride=FOLD), :]
        back = wide[pl.ds(j, LANES, stride=FOLD), :]
        out_ref[j * LANES : (j + 1) * LANES, 0:LANES] = (here * -2.0).astype(BF16)
        out_ref[j * LANES : (j + 1) * LANES, LANES:] = (back * 2.0).astype(BF16)


def join_kernel(info_ref, got_ref, right, out_ref, tail, prod0, prod1, extra, gates, bias):
    sub = lax.broadcasted_iota(jnp.int32, (SUBS, LANES), 0)
    lane = lax.broadcasted_iota(jnp.int32, (SUBS, LANES), 1)
    me = info_ref[0]

    def fill(k, _):
        extra[pl.ds(pl.multiple_of(k * SUBS, SUBS), SUBS), :] = got_ref[k, 2 * CHUNK : SLOT2, :].astype(F32)
        return 0

    lax.fori_loop(0, DEVS, fill, 0, unroll=16)

    def follow(k, _):
        x = got_ref[k, 0:CHUNK, :].astype(F32)
        halves = []
        for half in range(2):
            behind1 = extra[pl.ds(k * SUBS + 4 + half, SUBS, stride=0), :]
            behind2 = extra[pl.ds(k * SUBS + 6 + half, SUBS, stride=0), :]
            moved = pltpu.roll(x[half * SUBS : (half + 1) * SUBS], SUBS - 2, 0)
            halves.append(jnp.where(sub == SUBS - 2, behind1, jnp.where(sub == SUBS - 1, behind2, moved)))
        y = jnp.concatenate(halves, 0)
        tail[pl.ds(pl.multiple_of(k * CHUNK, CHUNK), CHUNK), :] = y.astype(BF16)
        return 0

    lax.fori_loop(0, SPAN // 2, follow, 0, unroll=4)

    row = lax.broadcasted_iota(jnp.int32, (STEP, LANES), 0)
    column = lax.broadcasted_iota(jnp.int32, (STEP, LANES), 1)
    place = STEP * column + row

    def band(offset):
        gap = 2 * column + offset - row
        return jnp.where((gap >= 1) & (gap < SPAN), 1.0, 0.0).astype(BF16)

    bands = jnp.concatenate([band(0), band(1), band(STEP), band(STEP + 1)], 1)
    closed = []
    for part in range(2):
        even = extra[pl.ds(2 * part, DEVS, stride=SUBS), :]
        odd = extra[pl.ds(2 * part + 1, DEVS, stride=SUBS), :]
        marks = jnp.concatenate(
            [even, odd, pltpu.roll(even, LANES - 1, 1), pltpu.roll(odd, LANES - 1, 1)], 0
        ).astype(BF16)
        crossed = jnp.dot(bands, marks, preferred_element_type=F32)
        valid, crossing = info_ref[3 + part], info_ref[5 + part]
        live = ((place + (SPAN - 1) < valid) | (crossing > 0)) & (crossed < 0.5)
        closed.append(jnp.where(live, 0.0, DEAD))
    to_even = (column & 1) == 0
    gates[0:STEP, :] = jnp.where(to_even, closed[0], pltpu.roll(closed[1], 1, 1))
    gates[STEP : 2 * STEP, :] = jnp.where(to_even, pltpu.roll(closed[0], LANES - 1, 1), closed[1])

    def pair(u):
        if u < STEP:
            rows = got_ref[u // 2, 0:CHUNK, :]
        elif u < 2 * STEP:
            rows = got_ref[(u - STEP) // 2, CHUNK : 2 * CHUNK, :]
        else:
            at = (u - 2 * STEP) // 2 * CHUNK
            rows = tail[at : at + CHUNK, :]
        x = rows.astype(F32)
        return x * x

    def source(b):
        per = BLOCK // CHUNK
        if b < DEVS // per:
            return got_ref[b * per : (b + 1) * per, 0:CHUNK, :].reshape(BLOCK, LANES)
        b -= DEVS // per
        if b < DEVS // per:
            return got_ref[b * per : (b + 1) * per, CHUNK : 2 * CHUNK, :].reshape(BLOCK, LANES)
        b -= DEVS // per
        return tail[b * BLOCK : (b + 1) * BLOCK, :]

    base = FOLD * lane - 2 * STEP * (sub >> 1)
    partner = jnp.where((sub & 1) == 0, info_ref[1], info_ref[2])
    ahead = jnp.where(partner == me + 1, base, -(2**20))
    behind = jnp.where(partner == me - 1, base, 2**20)
    limit = SEG - SPAN // 2

    def dot(b, prod):
        past = b - SPAN * SUBS // BLOCK
        rows, depth = source(b), LANES
        if past >= 0:
            rows, depth = jnp.concatenate([rows, source(past)], 1), 2 * LANES
        prod[...] = lax.dot_general(
            rows, right[:, 0:depth], (((1,), (1,)), ((), ())), preferred_element_type=F32
        )

    steps = BLOCK // SUBS
    count = 2 * STEP
    blocks = (count + SPAN) // steps

    def norms(energy, first, last):
        for i in range(first, last):
            gate = jnp.where(sub == lane, gates[pl.ds(i, SUBS, stride=0), :], 0.0)
            flat = jnp.sum(energy + gate, axis=1, keepdims=True)
            bias[i * SUBS : (i + 1) * SUBS, :] = jnp.broadcast_to(flat, (SUBS, LANES))
            at = slice(i % 2 * SUBS, (i % 2 + 1) * SUBS)
            energy = energy + (pair(i + SPAN)[at] - pair(i)[at])
        return energy

    total = [jnp.zeros((SUBS, LANES), F32) for _ in range(FOLD)]
    low = [jnp.full((SUBS, LANES), 3.0e38, F32) for _ in range(FOLD)]
    prods = (prod0, prod1)
    dot(0, prods[0])
    energy = jnp.zeros((SUBS, LANES), F32)
    for u in range(0, SPAN, 2):
        both = pair(u)
        energy = energy + (both[0:SUBS] + both[SUBS:])
    made = 0
    for b in range(blocks):
        if b + 1 < blocks:
            dot(b + 1, prods[(b + 1) % 2])
        goal = min((b + 1) * steps - (SPAN - 1) + (steps if EARLY else 0), count)
        if goal > made:
            energy = norms(energy, made, goal)
            made = goal
        prod = prods[b % 2]
        for r in range(steps):
            i = b * steps + r - (SPAN - 1)
            if i >= count:
                break
            total = [pltpu.roll(total[-1], 1, 1)] + total[:-1]
            rows = slice(r * SUBS, (r + 1) * SUBS)
            total = [total[j] + prod[rows, j * LANES : (j + 1) * LANES] for j in range(FOLD)]
            if i < 0:
                continue
            add = bias[i * SUBS : (i + 1) * SUBS, :]
            for j in range(FOLD):
                value = total[j] + add
                offset = j - (SPAN - 1) - i
                if i < SPAN // 2 - 1:
                    value = jnp.where(ahead > limit - offset, 3.0e38, value)
                if i > count - SPAN // 2:
                    value = jnp.where(behind < -limit - offset, 3.0e38, value)
                low[j] = jnp.minimum(low[j], value)

    for j in range(FOLD):
        out_ref[j : j + 1, :] = jnp.min(low[j], axis=0, keepdims=True)


def window_sum(values, count):
    total = values[0:count]
    for shift in range(1, SPAN):
        total = total + values[shift : shift + count]
    return total


def per_device(beats, track_marks, valid_beats, pairing):
    me = lax.axis_index("row") * lax.axis_size("col") + lax.axis_index("col")

    def room(mib):
        return pltpu.CompilerParams(vmem_limit_bytes=mib * 2**20)

    vmem = pl.BlockSpec(memory_space=VMEM)
    smem = pl.BlockSpec(memory_space=pltpu.SMEM)

    sent = pl.pallas_call(
        scatter_kernel,
        out_shape=jax.ShapeDtypeStruct((DEVS, SLOT, LANES), BF16),
        in_specs=[vmem] * 2,
        out_specs=vmem,
        scratch_shapes=[VMEM((SEG + 2 * LANES + SUBS, LANES), F32), VMEM((CHUNK, LANES), F32)],
        compiler_params=room(56),
    )(beats, track_marks.reshape(CHUNK, LANES))
    sent, beats, track_marks = lax.optimization_barrier((sent, beats, track_marks))
    spread = lax.all_to_all(sent, ("row", "col"), 0, 0, tiled=True)

    heads = jnp.concatenate([beats[:SPAN], jnp.broadcast_to(track_marks[None, :LANES].astype(BF16), (SUBS, LANES))], 0)
    head = lax.ppermute(heads, ("row", "col"), [(i + 1, i) for i in range(DEVS - 1)])
    right = pl.pallas_call(
        own_kernel,
        out_shape=jax.ShapeDtypeStruct((WRAP, 2 * LANES), BF16),
        in_specs=[vmem] * 2,
        out_specs=vmem,
        scratch_shapes=[VMEM((SEG + 3 * SPAN, LANES), F32)],
        compiler_params=room(16),
    )(beats, head)
    own_sq = jnp.concatenate(
        [
            jnp.sum(jnp.square(beats.astype(F32)), axis=1),
            jnp.sum(jnp.square(head[:SPAN].astype(F32)), axis=1),
        ],
        0,
    )
    norm = window_sum(own_sq, SEG)
    marks = jnp.concatenate([track_marks.astype(F32), head[SPAN, :SPAN].astype(F32)], 0)
    crossed = marks[1 : 1 + SEG]
    for shift in range(2, SPAN):
        crossed = crossed + marks[shift : shift + SEG]
    offsets = jnp.arange(SEG, dtype=jnp.int32)
    within = offsets + (SPAN - 1) < valid_beats[me]
    over = (valid_beats[me] == SEG) & (me < DEVS - 1)
    live = (within | over) & (crossed < 0.5)
    norm = jnp.where(live, norm, DEAD)

    partners = pairing[:, me]
    valid = valid_beats[partners]
    crossing = ((valid == SEG) & (partners < DEVS - 1)).astype(jnp.int32)
    after = jnp.minimum(pairing + 1, DEVS - 1)
    info = jnp.concatenate([me[None].astype(jnp.int32), partners, valid, crossing], 0)
    picks = jnp.concatenate([pairing, after], 0)


    routed = pl.pallas_call(
        route_kernel,
        out_shape=jax.ShapeDtypeStruct((DEVS, SLOT2, LANES), BF16),
        in_specs=[smem, vmem, smem] + [pl.BlockSpec(memory_space=pl.ANY)] * 2,
        out_specs=vmem,
        compiler_params=room(16),
    )(picks, spread, info, right, norm)
    got = lax.all_to_all(routed, ("row", "col"), 0, 0, tiled=True)
    best = pl.pallas_call(
        join_kernel,
        out_shape=jax.ShapeDtypeStruct((FOLD, LANES), F32),
        in_specs=[smem] + [vmem] * 2,
        out_specs=vmem,
        scratch_shapes=[
            VMEM((SPAN * SUBS, LANES), BF16),
            VMEM((BLOCK, WRAP), F32),
            VMEM((BLOCK, WRAP), F32),
            VMEM((DEVS * SUBS + SUBS, LANES), F32),
            VMEM((2 * STEP + SUBS, LANES), F32),
            VMEM((2 * SEG, LANES), F32),
        ],
        compiler_params=room(36),
    )(info, got, right)
    flat = best.T.reshape(WRAP)[SPAN - 1 : SPAN - 1 + SEG]
    return jnp.minimum((norm + flat) * (1.0 / (SPAN * WIDTH)), CEIL)


def solution(mesh):
    placed = (P(("row", "col"), None), P(("row", "col")), P(), P())
    return jax.shard_map(
        per_device, mesh=mesh, in_specs=placed, out_specs=P(("row", "col")), check_vma=False
    )
```

```python
import functools

import jax
import jax.numpy as jnp
from jax import lax
from jax.experimental import pallas as pl
from jax.experimental.pallas import tpu as pltpu
from jax.sharding import PartitionSpec as P

WIDTH = 128
SPAN = 64
CEIL = 4.0
SEG = 2048
DEVS = 128
LANES = 128
SUBS = 8
STEP = SEG // SUBS
FOLD = 17
WRAP = FOLD * LANES
CHUNK = 16
SLOT = 24
SLOT2 = 40
BLOCK = 256
DEAD = float(2**24)
F32 = jnp.float32
BF16 = jnp.bfloat16
VMEM = pltpu.VMEM


def scatter_kernel(beats_ref, marks_ref, out_ref, wide, flags):
    wide[0:SEG, :] = beats_ref[...].astype(F32)
    marks = marks_ref[...].astype(F32)
    flags[...] = marks
    pad = jnp.zeros((LANES - 2 * SUBS, LANES), F32)
    sub = lax.broadcasted_iota(jnp.int32, (SUBS, LANES), 0)
    turned = []
    for half in range(2):
        block = flags[pl.ds(half, SUBS, stride=2), :]
        extra = jnp.where(sub == 0, block, 0.0)
        turned.append(jnp.transpose(jnp.concatenate([block, extra, pad], 0)))
    flags2 = jnp.concatenate(turned, 0)
    out_ref[:, CHUNK:SLOT, :] = jnp.zeros((DEVS, SUBS, LANES), BF16)
    wide[pl.ds(SEG, 2 * LANES), :] = flags2

    def one(k, _):
        first = wide[pl.ds(2 * k, SUBS, stride=STEP), :]
        second = wide[pl.ds(2 * k + 1, SUBS, stride=STEP), :]
        out_ref[k, 0:CHUNK, :] = jnp.concatenate([first, second], 0).astype(BF16)
        mark0 = wide[pl.ds(SEG + 2 * k, SUBS, stride=0), :]
        mark1 = wide[pl.ds(SEG + 2 * k + 1, SUBS, stride=0), :]
        beat0 = wide[pl.ds(2 * k, SUBS, stride=0), :]
        beat1 = wide[pl.ds(2 * k + 1, SUBS, stride=0), :]
        even = jnp.where(sub < 4, mark0, beat0)
        odd = jnp.where(sub < 4, mark1, beat1)
        rest = jnp.where((sub & 1) == 0, even, odd)
        out_ref[k, CHUNK:SLOT, :] = rest.astype(BF16)
        return 0

    lax.fori_loop(0, DEVS, one, 0, unroll=16)


def route_kernel(pick_ref, got_ref, info_ref, right_ref, norm_ref, out_ref):
    sub = lax.broadcasted_iota(jnp.int32, (SUBS, LANES), 0)
    lane = lax.broadcasted_iota(jnp.int32, (SUBS, LANES), 1)
    marks = (sub < 4) & (lane < SUBS)
    to_first = (sub < 2) | (sub == 4) | (sub == 5)
    to_even = (sub & 1) == 0

    def one(d, _):
        first, second = pick_ref[0, d], pick_ref[1, d]
        after1, after2 = pick_ref[2, d], pick_ref[3, d]
        x = got_ref[first, 0:CHUNK, :].astype(F32)
        y = got_ref[second, 0:CHUNK, :].astype(F32)
        near, far = [], []
        for half in range(2):
            rows = slice(half * SUBS, (half + 1) * SUBS)
            near.append(jnp.where(to_even, x[rows], pltpu.roll(y[rows], 1, 0)))
            far.append(jnp.where(to_even, pltpu.roll(x[rows], SUBS - 1, 0), y[rows]))
        out_ref[d, 0:CHUNK, :] = jnp.concatenate(near, 0).astype(BF16)
        out_ref[d, CHUNK : 2 * CHUNK, :] = jnp.concatenate(far, 0).astype(BF16)
        mark1 = got_ref[first, CHUNK:SLOT, :].astype(F32)
        mark2 = got_ref[second, CHUNK:SLOT, :].astype(F32)
        next1 = got_ref[after1, CHUNK:SLOT, :].astype(F32)
        next2 = got_ref[after2, CHUNK:SLOT, :].astype(F32)
        own = jnp.where(to_first, mark1, mark2)
        behind = jnp.where(to_first, next1, next2)
        out_ref[d, 2 * CHUNK : SLOT2, :] = jnp.where(marks, own, behind).astype(BF16)
        return 0

    lax.fori_loop(0, DEVS, one, 0, unroll=4)


def own_kernel(own_ref, head_ref, out_ref, wide):
    wide[0:SPAN, :] = jnp.zeros((SPAN, LANES), F32)
    wide[pl.ds(SPAN, SEG), :] = own_ref[...].astype(F32)
    wide[pl.ds(SPAN + SEG, SPAN), :] = head_ref[0:SPAN, :].astype(F32)
    wide[pl.ds(2 * SPAN + SEG, SPAN), :] = jnp.zeros((SPAN, LANES), F32)
    for j in range(FOLD):
        here = wide[pl.ds(SPAN + j, LANES, stride=FOLD), :]
        back = wide[pl.ds(j, LANES, stride=FOLD), :]
        out_ref[j * LANES : (j + 1) * LANES, 0:LANES] = (here * -2.0).astype(BF16)
        out_ref[j * LANES : (j + 1) * LANES, LANES:] = (back * 2.0).astype(BF16)


def join_kernel(info_ref, got_ref, right, out_ref, tail, prod0, prod1, extra, gates, bias):
    sub = lax.broadcasted_iota(jnp.int32, (SUBS, LANES), 0)
    lane = lax.broadcasted_iota(jnp.int32, (SUBS, LANES), 1)
    me = info_ref[0]

    def fill(k, _):
        extra[pl.ds(pl.multiple_of(k * SUBS, SUBS), SUBS), :] = got_ref[k, 2 * CHUNK : SLOT2, :].astype(F32)
        return 0

    lax.fori_loop(0, DEVS, fill, 0, unroll=16)

    def follow(k, _):
        x = got_ref[k, 0:CHUNK, :].astype(F32)
        halves = []
        for half in range(2):
            behind1 = extra[pl.ds(k * SUBS + 4 + half, SUBS, stride=0), :]
            behind2 = extra[pl.ds(k * SUBS + 6 + half, SUBS, stride=0), :]
            moved = pltpu.roll(x[half * SUBS : (half + 1) * SUBS], SUBS - 2, 0)
            halves.append(jnp.where(sub == SUBS - 2, behind1, jnp.where(sub == SUBS - 1, behind2, moved)))
        y = jnp.concatenate(halves, 0)
        tail[pl.ds(pl.multiple_of(k * CHUNK, CHUNK), CHUNK), :] = y.astype(BF16)
        return 0

    lax.fori_loop(0, SPAN // 2, follow, 0, unroll=4)

    row = lax.broadcasted_iota(jnp.int32, (STEP, LANES), 0)
    column = lax.broadcasted_iota(jnp.int32, (STEP, LANES), 1)
    place = STEP * column + row

    def band(offset):
        gap = 2 * column + offset - row
        return jnp.where((gap >= 1) & (gap < SPAN), 1.0, 0.0).astype(BF16)

    bands = jnp.concatenate([band(0), band(1), band(STEP), band(STEP + 1)], 1)
    closed = []
    for part in range(2):
        even = extra[pl.ds(2 * part, DEVS, stride=SUBS), :]
        odd = extra[pl.ds(2 * part + 1, DEVS, stride=SUBS), :]
        marks = jnp.concatenate(
            [even, odd, pltpu.roll(even, LANES - 1, 1), pltpu.roll(odd, LANES - 1, 1)], 0
        ).astype(BF16)
        crossed = jnp.dot(bands, marks, preferred_element_type=F32)
        valid, crossing = info_ref[3 + part], info_ref[5 + part]
        live = ((place + (SPAN - 1) < valid) | (crossing > 0)) & (crossed < 0.5)
        closed.append(jnp.where(live, 0.0, DEAD))
    to_even = (column & 1) == 0
    gates[0:STEP, :] = jnp.where(to_even, closed[0], pltpu.roll(closed[1], 1, 1))
    gates[STEP : 2 * STEP, :] = jnp.where(to_even, pltpu.roll(closed[0], LANES - 1, 1), closed[1])

    def pair(u):
        if u < STEP:
            rows = got_ref[u // 2, 0:CHUNK, :]
        elif u < 2 * STEP:
            rows = got_ref[(u - STEP) // 2, CHUNK : 2 * CHUNK, :]
        else:
            at = (u - 2 * STEP) // 2 * CHUNK
            rows = tail[at : at + CHUNK, :]
        x = rows.astype(F32)
        return x * x

    def source(b):
        per = BLOCK // CHUNK
        if b < DEVS // per:
            return got_ref[b * per : (b + 1) * per, 0:CHUNK, :].reshape(BLOCK, LANES)
        b -= DEVS // per
        if b < DEVS // per:
            return got_ref[b * per : (b + 1) * per, CHUNK : 2 * CHUNK, :].reshape(BLOCK, LANES)
        b -= DEVS // per
        return tail[b * BLOCK : (b + 1) * BLOCK, :]

    base = FOLD * lane - 2 * STEP * (sub >> 1)
    partner = jnp.where((sub & 1) == 0, info_ref[1], info_ref[2])
    ahead = jnp.where(partner == me + 1, base, -(2**20))
    behind = jnp.where(partner == me - 1, base, 2**20)
    limit = SEG - SPAN // 2

    def dot(b, prod):
        past = b - SPAN * SUBS // BLOCK
        rows, depth = source(b), LANES
        if past >= 0:
            rows, depth = jnp.concatenate([rows, source(past)], 1), 2 * LANES
        prod[...] = lax.dot_general(
            rows, right[:, 0:depth], (((1,), (1,)), ((), ())), preferred_element_type=F32
        )

    steps = BLOCK // SUBS
    count = 2 * STEP
    blocks = (count + SPAN) // steps

    def norms(energy, first, last):
        for i in range(first, last):
            gate = jnp.where(sub == lane, gates[pl.ds(i, SUBS, stride=0), :], 0.0)
            flat = jnp.sum(energy + gate, axis=1, keepdims=True)
            bias[i * SUBS : (i + 1) * SUBS, :] = jnp.broadcast_to(flat, (SUBS, LANES))
            at = slice(i % 2 * SUBS, (i % 2 + 1) * SUBS)
            energy = energy + (pair(i + SPAN)[at] - pair(i)[at])
        return energy

    total = [jnp.zeros((SUBS, LANES), F32) for _ in range(FOLD)]
    low = [jnp.full((SUBS, LANES), 3.0e38, F32) for _ in range(FOLD)]
    prods = (prod0, prod1)
    dot(0, prods[0])
    energy = jnp.zeros((SUBS, LANES), F32)
    for u in range(0, SPAN, 2):
        both = pair(u)
        energy = energy + (both[0:SUBS] + both[SUBS:])
    made = 0
    for b in range(blocks):
        if b + 1 < blocks:
            dot(b + 1, prods[(b + 1) % 2])
        goal = min((b + 1) * steps - (SPAN - 1), count)
        if goal > made:
            energy = norms(energy, made, goal)
            made = goal
        prod = prods[b % 2]
        for r in range(steps):
            i = b * steps + r - (SPAN - 1)
            if i >= count:
                break
            total = [pltpu.roll(total[-1], 1, 1)] + total[:-1]
            rows = slice(r * SUBS, (r + 1) * SUBS)
            total = [total[j] + prod[rows, j * LANES : (j + 1) * LANES] for j in range(FOLD)]
            if i < 0:
                continue
            add = bias[i * SUBS : (i + 1) * SUBS, :]
            for j in range(FOLD):
                value = total[j] + add
                offset = j - (SPAN - 1) - i
                if i < SPAN // 2 - 1:
                    value = jnp.where(ahead > limit - offset, 3.0e38, value)
                if i > count - SPAN // 2:
                    value = jnp.where(behind < -limit - offset, 3.0e38, value)
                low[j] = jnp.minimum(low[j], value)

    for j in range(FOLD):
        out_ref[j : j + 1, :] = jnp.min(low[j], axis=0, keepdims=True)


def window_sum(values, count):
    total = values[0:count]
    for shift in range(1, SPAN):
        total = total + values[shift : shift + count]
    return total


def per_device(beats, track_marks, valid_beats, pairing):
    me = lax.axis_index("row") * lax.axis_size("col") + lax.axis_index("col")

    def room(mib):
        return pltpu.CompilerParams(vmem_limit_bytes=mib * 2**20)

    vmem = pl.BlockSpec(memory_space=VMEM)
    smem = pl.BlockSpec(memory_space=pltpu.SMEM)

    sent = pl.pallas_call(
        scatter_kernel,
        out_shape=jax.ShapeDtypeStruct((DEVS, SLOT, LANES), BF16),
        in_specs=[vmem] * 2,
        out_specs=vmem,
        scratch_shapes=[VMEM((SEG + 2 * LANES + SUBS, LANES), F32), VMEM((CHUNK, LANES), F32)],
        compiler_params=room(56),
    )(beats, track_marks.reshape(CHUNK, LANES))
    sent, beats, track_marks = lax.optimization_barrier((sent, beats, track_marks))
    spread = lax.all_to_all(sent, ("row", "col"), 0, 0, tiled=True)

    heads = jnp.concatenate([beats[:SPAN], jnp.broadcast_to(track_marks[None, :LANES].astype(BF16), (SUBS, LANES))], 0)
    head = lax.ppermute(heads, ("row", "col"), [(i + 1, i) for i in range(DEVS - 1)])
    right = pl.pallas_call(
        own_kernel,
        out_shape=jax.ShapeDtypeStruct((WRAP, 2 * LANES), BF16),
        in_specs=[vmem] * 2,
        out_specs=vmem,
        scratch_shapes=[VMEM((SEG + 3 * SPAN, LANES), F32)],
        compiler_params=room(16),
    )(beats, head)
    own_sq = jnp.concatenate(
        [
            jnp.sum(jnp.square(beats.astype(F32)), axis=1),
            jnp.sum(jnp.square(head[:SPAN].astype(F32)), axis=1),
        ],
        0,
    )
    norm = window_sum(own_sq, SEG)
    marks = jnp.concatenate([track_marks.astype(F32), head[SPAN, :SPAN].astype(F32)], 0)
    crossed = marks[1 : 1 + SEG]
    for shift in range(2, SPAN):
        crossed = crossed + marks[shift : shift + SEG]
    offsets = jnp.arange(SEG, dtype=jnp.int32)
    within = offsets + (SPAN - 1) < valid_beats[me]
    over = (valid_beats[me] == SEG) & (me < DEVS - 1)
    live = (within | over) & (crossed < 0.5)
    norm = jnp.where(live, norm, DEAD)

    partners = pairing[:, me]
    valid = valid_beats[partners]
    crossing = ((valid == SEG) & (partners < DEVS - 1)).astype(jnp.int32)
    after = jnp.minimum(pairing + 1, DEVS - 1)
    info = jnp.concatenate([me[None].astype(jnp.int32), partners, valid, crossing], 0)
    picks = jnp.concatenate([pairing, after], 0)


    routed = pl.pallas_call(
        route_kernel,
        out_shape=jax.ShapeDtypeStruct((DEVS, SLOT2, LANES), BF16),
        in_specs=[smem, vmem, smem] + [pl.BlockSpec(memory_space=pl.ANY)] * 2,
        out_specs=vmem,
        compiler_params=room(16),
    )(picks, spread, info, right, norm)
    got = lax.all_to_all(routed, ("row", "col"), 0, 0, tiled=True)
    best = pl.pallas_call(
        join_kernel,
        out_shape=jax.ShapeDtypeStruct((FOLD, LANES), F32),
        in_specs=[smem] + [vmem] * 2,
        out_specs=vmem,
        scratch_shapes=[
            VMEM((SPAN * SUBS, LANES), BF16),
            VMEM((BLOCK, WRAP), F32),
            VMEM((BLOCK, WRAP), F32),
            VMEM((DEVS * SUBS + SUBS, LANES), F32),
            VMEM((2 * STEP + SUBS, LANES), F32),
            VMEM((2 * SEG, LANES), F32),
        ],
        compiler_params=room(36),
    )(info, got, right)
    flat = best.T.reshape(WRAP)[SPAN - 1 : SPAN - 1 + SEG]
    return jnp.minimum((norm + flat) * (1.0 / (SPAN * WIDTH)), CEIL)


def solution(mesh):
    placed = (P(("row", "col"), None), P(("row", "col")), P(), P())
    return jax.shard_map(
        per_device, mesh=mesh, in_specs=placed, out_specs=P(("row", "col")), check_vma=False
    )
```

```python
import functools

import jax
import jax.numpy as jnp
from jax import lax
from jax.experimental import pallas as pl
from jax.experimental.pallas import tpu as pltpu
from jax.sharding import PartitionSpec as P

WIDTH = 128
SPAN = 64
CEIL = 4.0
SEG = 2048
DEVS = 128
LANES = 128
SUBS = 8
STEP = SEG // SUBS
FOLD = 17
WRAP = FOLD * LANES
CHUNK = 16
SLOT = 24
SLOT2 = 40
BLOCK = 256
DEAD = float(2**24)
F32 = jnp.float32
BF16 = jnp.bfloat16
VMEM = pltpu.VMEM


def scatter_kernel(beats_ref, marks_ref, out_ref, wide, flags):
    wide[0:SEG, :] = beats_ref[...].astype(F32)
    marks = marks_ref[...].astype(F32)
    flags[...] = marks
    pad = jnp.zeros((LANES - 2 * SUBS, LANES), F32)
    sub = lax.broadcasted_iota(jnp.int32, (SUBS, LANES), 0)
    turned = []
    for half in range(2):
        block = flags[pl.ds(half, SUBS, stride=2), :]
        extra = jnp.where(sub == 0, block, 0.0)
        turned.append(jnp.transpose(jnp.concatenate([block, extra, pad], 0)))
    flags2 = jnp.concatenate(turned, 0)
    wide[pl.ds(SEG, 2 * LANES), :] = flags2

    def one(k, _):
        first = wide[pl.ds(2 * k, SUBS, stride=STEP), :]
        second = wide[pl.ds(2 * k + 1, SUBS, stride=STEP), :]
        out_ref[k, 0:CHUNK, :] = jnp.concatenate([first, second], 0).astype(BF16)
        mark0 = wide[pl.ds(SEG + 2 * k, SUBS, stride=0), :]
        mark1 = wide[pl.ds(SEG + 2 * k + 1, SUBS, stride=0), :]
        beat0 = wide[pl.ds(2 * k, SUBS, stride=0), :]
        beat1 = wide[pl.ds(2 * k + 1, SUBS, stride=0), :]
        even = jnp.where(sub < 4, mark0, beat0)
        odd = jnp.where(sub < 4, mark1, beat1)
        rest = jnp.where((sub & 1) == 0, even, odd)
        out_ref[k, CHUNK:SLOT, :] = rest.astype(BF16)
        return 0

    lax.fori_loop(0, DEVS, one, 0, unroll=16)


def route_kernel(pick_ref, got_ref, info_ref, right_ref, norm_ref, out_ref):
    sub = lax.broadcasted_iota(jnp.int32, (SUBS, LANES), 0)
    lane = lax.broadcasted_iota(jnp.int32, (SUBS, LANES), 1)
    marks = (sub < 4) & (lane < SUBS)
    to_first = (sub < 2) | (sub == 4) | (sub == 5)
    to_even = (sub & 1) == 0

    def one(d, _):
        first, second = pick_ref[0, d], pick_ref[1, d]
        after1, after2 = pick_ref[2, d], pick_ref[3, d]
        x = got_ref[first, 0:CHUNK, :].astype(F32)
        y = got_ref[second, 0:CHUNK, :].astype(F32)
        near, far = [], []
        for half in range(2):
            rows = slice(half * SUBS, (half + 1) * SUBS)
            near.append(jnp.where(to_even, x[rows], pltpu.roll(y[rows], 1, 0)))
            far.append(jnp.where(to_even, pltpu.roll(x[rows], SUBS - 1, 0), y[rows]))
        out_ref[d, 0:CHUNK, :] = jnp.concatenate(near, 0).astype(BF16)
        out_ref[d, CHUNK : 2 * CHUNK, :] = jnp.concatenate(far, 0).astype(BF16)
        mark1 = got_ref[first, CHUNK:SLOT, :].astype(F32)
        mark2 = got_ref[second, CHUNK:SLOT, :].astype(F32)
        next1 = got_ref[after1, CHUNK:SLOT, :].astype(F32)
        next2 = got_ref[after2, CHUNK:SLOT, :].astype(F32)
        own = jnp.where(to_first, mark1, mark2)
        behind = jnp.where(to_first, next1, next2)
        out_ref[d, 2 * CHUNK : SLOT2, :] = jnp.where(marks, own, behind).astype(BF16)
        return 0

    lax.fori_loop(0, DEVS, one, 0, unroll=4)


def own_kernel(own_ref, head_ref, out_ref, bands_ref, wide):
    wide[0:SPAN, :] = jnp.zeros((SPAN, LANES), F32)
    wide[pl.ds(SPAN, SEG), :] = own_ref[...].astype(F32)
    wide[pl.ds(SPAN + SEG, SPAN), :] = head_ref[0:SPAN, :].astype(F32)
    wide[pl.ds(2 * SPAN + SEG, SPAN), :] = jnp.zeros((SPAN, LANES), F32)
    for j in range(FOLD):
        here = wide[pl.ds(SPAN + j, LANES, stride=FOLD), :]
        back = wide[pl.ds(j, LANES, stride=FOLD), :]
        out_ref[j * LANES : (j + 1) * LANES, 0:LANES] = (here * -2.0).astype(BF16)
        out_ref[j * LANES : (j + 1) * LANES, LANES:] = (back * 2.0).astype(BF16)

    row = lax.broadcasted_iota(jnp.int32, (STEP, LANES), 0)
    column = lax.broadcasted_iota(jnp.int32, (STEP, LANES), 1)

    def band(offset):
        gap = 2 * column + offset - row
        return jnp.where((gap >= 1) & (gap < SPAN), 1.0, 0.0).astype(BF16)

    bands_ref[...] = jnp.concatenate([band(0), band(1), band(STEP), band(STEP + 1)], 1)


def join_kernel(info_ref, got_ref, right, bands_ref, out_ref, tail, prod0, prod1, extra, gates, bias):
    sub = lax.broadcasted_iota(jnp.int32, (SUBS, LANES), 0)
    lane = lax.broadcasted_iota(jnp.int32, (SUBS, LANES), 1)
    me = info_ref[0]

    def fill(k, _):
        extra[pl.ds(pl.multiple_of(k * SUBS, SUBS), SUBS), :] = got_ref[k, 2 * CHUNK : SLOT2, :].astype(F32)
        return 0

    lax.fori_loop(0, DEVS, fill, 0, unroll=16)

    def follow(k, _):
        x = got_ref[k, 0:CHUNK, :].astype(F32)
        halves = []
        for half in range(2):
            behind1 = extra[pl.ds(k * SUBS + 4 + half, SUBS, stride=0), :]
            behind2 = extra[pl.ds(k * SUBS + 6 + half, SUBS, stride=0), :]
            moved = pltpu.roll(x[half * SUBS : (half + 1) * SUBS], SUBS - 2, 0)
            halves.append(jnp.where(sub == SUBS - 2, behind1, jnp.where(sub == SUBS - 1, behind2, moved)))
        y = jnp.concatenate(halves, 0)
        tail[pl.ds(pl.multiple_of(k * CHUNK, CHUNK), CHUNK), :] = y.astype(BF16)
        return 0

    lax.fori_loop(0, SPAN // 2, follow, 0, unroll=4)

    row = lax.broadcasted_iota(jnp.int32, (STEP, LANES), 0)
    column = lax.broadcasted_iota(jnp.int32, (STEP, LANES), 1)
    place = STEP * column + row

    bands = bands_ref[...]
    closed = []
    for part in range(2):
        even = extra[pl.ds(2 * part, DEVS, stride=SUBS), :]
        odd = extra[pl.ds(2 * part + 1, DEVS, stride=SUBS), :]
        marks = jnp.concatenate(
            [even, odd, pltpu.roll(even, LANES - 1, 1), pltpu.roll(odd, LANES - 1, 1)], 0
        ).astype(BF16)
        crossed = jnp.dot(bands, marks, preferred_element_type=F32)
        valid, crossing = info_ref[3 + part], info_ref[5 + part]
        live = ((place + (SPAN - 1) < valid) | (crossing > 0)) & (crossed < 0.5)
        closed.append(jnp.where(live, 0.0, DEAD))
    to_even = (column & 1) == 0
    gates[0:STEP, :] = jnp.where(to_even, closed[0], pltpu.roll(closed[1], 1, 1))
    gates[STEP : 2 * STEP, :] = jnp.where(to_even, pltpu.roll(closed[0], LANES - 1, 1), closed[1])

    def pair(u):
        if u < STEP:
            rows = got_ref[u // 2, 0:CHUNK, :]
        elif u < 2 * STEP:
            rows = got_ref[(u - STEP) // 2, CHUNK : 2 * CHUNK, :]
        else:
            at = (u - 2 * STEP) // 2 * CHUNK
            rows = tail[at : at + CHUNK, :]
        x = rows.astype(F32)
        return x * x

    def source(b):
        per = BLOCK // CHUNK
        if b < DEVS // per:
            return got_ref[b * per : (b + 1) * per, 0:CHUNK, :].reshape(BLOCK, LANES)
        b -= DEVS // per
        if b < DEVS // per:
            return got_ref[b * per : (b + 1) * per, CHUNK : 2 * CHUNK, :].reshape(BLOCK, LANES)
        b -= DEVS // per
        return tail[b * BLOCK : (b + 1) * BLOCK, :]

    base = FOLD * lane - 2 * STEP * (sub >> 1)
    partner = jnp.where((sub & 1) == 0, info_ref[1], info_ref[2])
    ahead = jnp.where(partner == me + 1, base, -(2**20))
    behind = jnp.where(partner == me - 1, base, 2**20)
    limit = SEG - SPAN // 2

    def dot(b, prod):
        past = b - SPAN * SUBS // BLOCK
        rows, depth = source(b), LANES
        if past >= 0:
            rows, depth = jnp.concatenate([rows, source(past)], 1), 2 * LANES
        prod[...] = lax.dot_general(
            rows, right[:, 0:depth], (((1,), (1,)), ((), ())), preferred_element_type=F32
        )

    steps = BLOCK // SUBS
    count = 2 * STEP
    blocks = (count + SPAN) // steps

    def norms(energy, first, last):
        for i in range(first, last):
            gate = jnp.where(sub == lane, gates[pl.ds(i, SUBS, stride=0), :], 0.0)
            flat = jnp.sum(energy + gate, axis=1, keepdims=True)
            bias[i * SUBS : (i + 1) * SUBS, :] = jnp.broadcast_to(flat, (SUBS, LANES))
            at = slice(i % 2 * SUBS, (i % 2 + 1) * SUBS)
            energy = energy + (pair(i + SPAN)[at] - pair(i)[at])
        return energy

    total = [jnp.zeros((SUBS, LANES), F32) for _ in range(FOLD)]
    low = [jnp.full((SUBS, LANES), 3.0e38, F32) for _ in range(FOLD)]
    prods = (prod0, prod1)
    dot(0, prods[0])
    energy = jnp.zeros((SUBS, LANES), F32)
    for u in range(0, SPAN, 2):
        both = pair(u)
        energy = energy + (both[0:SUBS] + both[SUBS:])
    made = 0
    for b in range(blocks):
        if b + 1 < blocks:
            dot(b + 1, prods[(b + 1) % 2])
        goal = min((b + 1) * steps - (SPAN - 1), count)
        if goal > made:
            energy = norms(energy, made, goal)
            made = goal
        prod = prods[b % 2]
        for r in range(steps):
            i = b * steps + r - (SPAN - 1)
            if i >= count:
                break
            total = [pltpu.roll(total[-1], 1, 1)] + total[:-1]
            rows = slice(r * SUBS, (r + 1) * SUBS)
            total = [total[j] + prod[rows, j * LANES : (j + 1) * LANES] for j in range(FOLD)]
            if i < 0:
                continue
            add = bias[i * SUBS : (i + 1) * SUBS, :]
            for j in range(FOLD):
                value = total[j] + add
                offset = j - (SPAN - 1) - i
                if i < SPAN // 2 - 1:
                    value = jnp.where(ahead > limit - offset, 3.0e38, value)
                if i > count - SPAN // 2:
                    value = jnp.where(behind < -limit - offset, 3.0e38, value)
                low[j] = jnp.minimum(low[j], value)

    for j in range(FOLD):
        out_ref[j : j + 1, :] = jnp.min(low[j], axis=0, keepdims=True)


def window_sum(values, count):
    total = values[0:count]
    for shift in range(1, SPAN):
        total = total + values[shift : shift + count]
    return total


def per_device(beats, track_marks, valid_beats, pairing):
    me = lax.axis_index("row") * lax.axis_size("col") + lax.axis_index("col")

    def room(mib):
        return pltpu.CompilerParams(vmem_limit_bytes=mib * 2**20)

    vmem = pl.BlockSpec(memory_space=VMEM)
    smem = pl.BlockSpec(memory_space=pltpu.SMEM)

    sent = pl.pallas_call(
        scatter_kernel,
        out_shape=jax.ShapeDtypeStruct((DEVS, SLOT, LANES), BF16),
        in_specs=[vmem] * 2,
        out_specs=vmem,
        scratch_shapes=[VMEM((SEG + 2 * LANES + SUBS, LANES), F32), VMEM((CHUNK, LANES), F32)],
        compiler_params=room(56),
    )(beats, track_marks.reshape(CHUNK, LANES))
    sent, beats, track_marks = lax.optimization_barrier((sent, beats, track_marks))
    spread = lax.all_to_all(sent, ("row", "col"), 0, 0, tiled=True)

    heads = jnp.concatenate([beats[:SPAN], jnp.broadcast_to(track_marks[None, :LANES].astype(BF16), (SUBS, LANES))], 0)
    head = lax.ppermute(heads, ("row", "col"), [(i + 1, i) for i in range(DEVS - 1)])
    right, bands = pl.pallas_call(
        own_kernel,
        out_shape=(
            jax.ShapeDtypeStruct((WRAP, 2 * LANES), BF16),
            jax.ShapeDtypeStruct((STEP, 4 * LANES), BF16),
        ),
        in_specs=[vmem] * 2,
        out_specs=(vmem, vmem),
        scratch_shapes=[VMEM((SEG + 3 * SPAN, LANES), F32)],
        compiler_params=room(16),
    )(beats, head)
    own_sq = jnp.concatenate(
        [
            jnp.sum(jnp.square(beats.astype(F32)), axis=1),
            jnp.sum(jnp.square(head[:SPAN].astype(F32)), axis=1),
        ],
        0,
    )
    norm = window_sum(own_sq, SEG)
    marks = jnp.concatenate([track_marks.astype(F32), head[SPAN, :SPAN].astype(F32)], 0)
    crossed = marks[1 : 1 + SEG]
    for shift in range(2, SPAN):
        crossed = crossed + marks[shift : shift + SEG]
    offsets = jnp.arange(SEG, dtype=jnp.int32)
    within = offsets + (SPAN - 1) < valid_beats[me]
    over = (valid_beats[me] == SEG) & (me < DEVS - 1)
    live = (within | over) & (crossed < 0.5)
    norm = jnp.where(live, norm, DEAD)

    partners = pairing[:, me]
    valid = valid_beats[partners]
    crossing = ((valid == SEG) & (partners < DEVS - 1)).astype(jnp.int32)
    after = jnp.minimum(pairing + 1, DEVS - 1)
    info = jnp.concatenate([me[None].astype(jnp.int32), partners, valid, crossing], 0)
    picks = jnp.concatenate([pairing, after], 0)


    routed = pl.pallas_call(
        route_kernel,
        out_shape=jax.ShapeDtypeStruct((DEVS, SLOT2, LANES), BF16),
        in_specs=[smem, vmem, smem] + [pl.BlockSpec(memory_space=pl.ANY)] * 2,
        out_specs=vmem,
        compiler_params=room(16),
    )(picks, spread, info, right, norm)
    got = lax.all_to_all(routed, ("row", "col"), 0, 0, tiled=True)
    best = pl.pallas_call(
        join_kernel,
        out_shape=jax.ShapeDtypeStruct((FOLD, LANES), F32),
        in_specs=[smem] + [vmem] * 3,
        out_specs=vmem,
        scratch_shapes=[
            VMEM((SPAN * SUBS, LANES), BF16),
            VMEM((BLOCK, WRAP), F32),
            VMEM((BLOCK, WRAP), F32),
            VMEM((DEVS * SUBS + SUBS, LANES), F32),
            VMEM((2 * STEP + SUBS, LANES), F32),
            VMEM((2 * SEG, LANES), F32),
        ],
        compiler_params=room(36),
    )(info, got, right, bands)
    flat = best.T.reshape(WRAP)[SPAN - 1 : SPAN - 1 + SEG]
    return jnp.minimum((norm + flat) * (1.0 / (SPAN * WIDTH)), CEIL)


def solution(mesh):
    placed = (P(("row", "col"), None), P(("row", "col")), P(), P())
    return jax.shard_map(
        per_device, mesh=mesh, in_specs=placed, out_specs=P(("row", "col")), check_vma=False
    )
```
